32 devices in a mesh: slab: 8 (over z, y), tile: 4 (over x, core).
Axes of the slice: x: 2, y: 2, z: 4, core: 2. Of those that a mesh axis runs over, the one named last changes fastest.
Arguments:
- grid: bfloat16 [64, 256, 1024], P('slab', 'tile'), may hold values from -6 to 6
- type_table: float32 [16, 8], replicated, may hold values from -4 to 4
- counts: int32 [512], P(('slab', 'tile')), may hold values from 10 to 120
- types: int32 [512, 128], P(('slab', 'tile')), may hold values from 0 to 15
- offsets: float32 [512, 3, 128], P(('slab', 'tile')), may hold values from 0 to 0.999
- route: int32 [512, 1], P('slab'), may hold values from 0 to 7; in each aligned block of 64 rows (0 to 63, 64 to 127, ...) at most 16 rows name the same one
- base_y: int32 [512], P(('slab', 'tile')), may hold values from 0 to 223
- base_z: int32 [512], P(('slab', 'tile')), may hold values from 0 to 95
Outputs:
- energy: float32 [512], P(('slab', 'tile'))
The draws below stay inside these ranges and needn't reach their ends.
Inputs may be any that keep to these rules, and one draw needn't show every extreme that they name: `route`: among the rows of one aligned block of 64 poses (those starting on one group of tile devices), at most 16 name the same slab.
All inputs are finite; a program needn't handle non-finite values.
Results may differ from the reference program's by a relative error of at most 0.0003.
Values may be sent and summed in bfloat16 or wider, within the bound.
A program may use at most 64 MiB of HBM per device.

```python
import math
import jax
import jax.numpy as jnp
import numpy as np

CH = 8
TYPES = 16
ATOMS = 128
SPAN = 32
CX = 8
NZ = 128
POSE_DEV = 16
NX = 64
NY = 256
POSES = 512
SLOT_CAP = 16
N_SLAB = 8


def plant(drawn, own_key, least, top_value):
    extent = drawn.shape
    place = [jax.random.randint(jax.random.fold_in(own_key, axis), (), 0, extent[axis]) for axis in range(len(extent))]
    drawn = drawn.at[tuple(place)].set(least)
    longest = extent.index(max(extent))
    place[longest] = (place[longest] + 1) % extent[longest]
    return drawn.at[tuple(place)].set(top_value)


def steps_of(own_key, extent, pieces, low, top_value):
    level, own = 1.0, jax.random.fold_in(own_key, 6)
    for axis_at, parts in pieces:
        heights = jnp.exp(jax.random.uniform(jax.random.fold_in(own, axis_at), (parts,), jnp.float32, low / len(pieces), top_value / len(pieces)))
        level = level * jnp.repeat(heights, extent[axis_at] // parts).reshape([-1 if axis == axis_at else 1 for axis in range(len(extent))])
    return level


def assign_block(key, own, number, rows, number_of, top, bound, slope):
    ranking = jax.random.permutation(key, number_of)
    crowded, common = portions_of(number_of, rows * top, bound, slope, True), portions_of(number_of, rows * top, bound, slope, False)
    places = jnp.arange(number_of)

    def named(tallies, turn):
        used = int((tallies > 0).sum())
        fixed = max(1, used // 4)
        moved = fixed + (places - fixed + turn * (used - fixed)) % max(1, number_of - fixed)
        return jnp.zeros((number_of,), jnp.int32).at[ranking[jnp.where(places < fixed, places, moved)]].set(jnp.asarray(tallies, jnp.int32))

    tallies = jnp.where(number % 4 == 0, named(crowded, number // 4), named(common, number - number // 4 - 1))
    mixed = jax.random.permutation(jax.random.fold_in(own, 3), number_of)
    giver, taker = mixed[0:number_of // 2 * 2:2], mixed[1:number_of // 2 * 2:2]
    margin = jnp.minimum(tallies[giver] - 1, bound - tallies[taker]) // 2
    margin = jnp.where((giver == ranking[0]) | (taker == ranking[0]) | (tallies[taker] == 0), 0, jnp.maximum(margin, 0))
    moved = jax.random.randint(jax.random.fold_in(own, 4), (number_of // 2,), 0, 1 << 20) % (margin + 1)
    tallies = tallies.at[giver].add(-moved).at[taker].add(moved)
    members = jnp.searchsorted(jnp.cumsum(tallies), jnp.arange(rows * top), side="right").astype(jnp.int32)
    table = members.reshape(top, rows).T
    table = table[jax.random.permutation(jax.random.fold_in(own, 1), rows)]
    turn = jax.random.randint(jax.random.fold_in(own, 2), (rows, 1), 0, top)
    return jnp.take_along_axis(table, (jnp.arange(top)[None, :] + turn) % top, axis=1)


def portions_of(count, total, reach, skew, full):
    weights = [(1 << 20) // math.isqrt(grade ** skew) + 1 for grade in range(1, count + 1)]
    largest = reach if full else min(reach, max(-(-total // count), total * weights[0] // sum(weights)))
    least = 1 if total - largest >= count - 1 else 0
    holding, spare = [largest] + [least] * (count - 1), total - largest - least * (count - 1)
    while spare > 0:
        free = [i for i in range(1, count) if holding[i] < largest] or [i for i in range(1, count) if holding[i] < reach]
        mass, remaining = sum([weights[i] for i in free]), spare
        for i in free:
            extra = min(reach - holding[i], max(1, remaining * weights[i] // mass), spare)
            holding[i] = holding[i] + extra
            spare = spare - extra
    return np.array(holding)


def scatter_about(stream_key, dims, spread, reach, split=(), dtype=jnp.bfloat16):
    values = jax.random.normal(stream_key, dims, jnp.float32) * spread
    if len(split) > 0:
        values = steps_of(stream_key, dims, split, -0.22, 0.18) * values
    return jnp.clip(values, min=-reach, max=reach).astype(dtype)


def setup_inputs(seed: int = 0) -> dict:
    splits = jax.random.split(jax.random.key(seed), 9)
    grid = scatter_about(splits[0], (NX, NY, NZ * CH), 1.0, 6.0, ((0, 8), (1, 4)))
    type_table = scatter_about(splits[1], (TYPES, CH), 1.0, 4.0, (), jnp.float32)
    counts = plant(jax.random.randint(splits[2], (POSES,), 10, 121), jax.random.fold_in(splits[2], 1), 10, 120).astype(jnp.int32)
    types = plant(jax.random.randint(splits[3], (POSES, ATOMS), 0, TYPES), jax.random.fold_in(splits[3], 1), 0, TYPES - 1).astype(jnp.int32)
    offsets = jnp.clip(0.999 * jax.random.uniform(splits[4], (POSES, 3, ATOMS), jnp.float32) ** steps_of(splits[4], (POSES, 3, ATOMS), ((0, 32),), -0.2, 0.2), 0.0, 0.999)
    route_keys = jax.random.split(jax.random.fold_in(splits[5], 1), POSES // (4 * POSE_DEV))
    route_turns = jax.random.permutation(jax.random.fold_in(splits[5], 3), POSES // (4 * POSE_DEV))
    route = jax.vmap(lambda own, number: assign_block(jax.random.fold_in(splits[5], 2), own, number, 4 * POSE_DEV, N_SLAB, 1, SLOT_CAP, 2))(route_keys, route_turns).reshape((POSES, 1))
    base_y = plant(jax.random.randint(splits[6], (POSES,), 0, NY - SPAN), jax.random.fold_in(splits[6], 1), 0, (NY - SPAN) - 1).astype(jnp.int32)
    base_z = plant(jax.random.randint(splits[7], (POSES,), 0, NZ - SPAN), jax.random.fold_in(splits[7], 1), 0, (NZ - SPAN) - 1).astype(jnp.int32)
    return {"grid": grid, "type_table": type_table, "counts": counts, "types": types, "offsets": offsets, "route": route, "base_y": base_y, "base_z": base_z}


def reference(grid, type_table, counts, types, offsets, route, base_y, base_z):
    local_x = offsets[:, 0, :] * (CX - 1)
    pos_y = base_y[:, None].astype(jnp.float32) + offsets[:, 1, :] * SPAN
    pos_z = base_z[:, None].astype(jnp.float32) + offsets[:, 2, :] * SPAN
    live = (jnp.arange(ATOMS)[None, :] < counts[:, None]).astype(jnp.float32) / counts[:, None].astype(jnp.float32)
    weights = type_table[types] * live[:, :, None]
    floor_x = jnp.floor(local_x)
    floor_y = jnp.floor(pos_y)
    floor_z = jnp.floor(pos_z)
    frac_x = local_x - floor_x
    frac_y = pos_y - floor_y
    frac_z = pos_z - floor_z
    cell_x = route[:, 0:1] * CX + floor_x.astype(jnp.int32)
    cell_y = floor_y.astype(jnp.int32)
    cell_z = floor_z.astype(jnp.int32)
    flat_grid = grid.reshape(NX * NY * NZ, CH)
    total = jnp.zeros(local_x.shape + (CH,), jnp.float32)
    for corner in range(8):
        step_x, step_y, step_z = corner // 4, (corner // 2) % 2, corner % 2
        factor = (frac_x if step_x else 1.0 - frac_x) * (frac_y if step_y else 1.0 - frac_y) * (frac_z if step_z else 1.0 - frac_z)
        index = ((cell_x + step_x) * NY + cell_y + step_y) * NZ + cell_z + step_z
        values = jnp.take(flat_grid, index, axis=0).astype(jnp.float32)
        total = total + factor[:, :, None] * values
    return jnp.sum(jnp.sum(total * weights, axis=2), axis=1)
```

```python
import functools

import jax
import jax.numpy as jnp
from jax import lax
from jax.experimental import pallas as pl
from jax.experimental.pallas import tpu as pltpu
from jax.sharding import PartitionSpec as P

SPAN = 32
ROWS = 4
FAR = -1.0e6
MESH = pl.DeviceIdType.MESH


def iota(shape, dim):
    return lax.broadcasted_iota(jnp.int32, shape, dim)


def to_row(col, count):
    eye = iota((count, count), 0) == iota((count, count), 1)
    return jnp.sum(jnp.where(eye, col, 0), axis=0, keepdims=True)


def exchange_kernel(
    slabs, tiles, cap, cells_x,
    counts_ref, base_y_ref, base_z_ref, route_ref, types_ref, offsets_ref,
    incoming_ref,
    gathered, outgoing, tile_send, tile_recv, slab_send, slab_recv,
):
    me_s = lax.axis_index("slab")
    me_t = lax.axis_index("tile")
    poses, atoms = types_ref.shape
    group = tiles * poses
    slots = slabs * cap

    barrier = pltpu.get_barrier_semaphore()
    for i in range(1, tiles):
        pl.semaphore_signal(
            barrier, inc=1, device_id=(me_s, lax.rem(me_t + i, tiles)), device_id_type=MESH
        )

    @pl.loop(1, slabs)
    def _(i):
        pl.semaphore_signal(
            barrier, inc=1, device_id=(lax.rem(me_s + i, slabs), me_t), device_id_type=MESH
        )

    lane = iota((1, atoms), 1)
    for p in range(poses):
        off = offsets_ref[p]
        by = jnp.full((1, atoms), base_y_ref[p], jnp.int32).astype(jnp.float32)
        bz = jnp.full((1, atoms), base_z_ref[p], jnp.int32).astype(jnp.float32)
        kind = jnp.where(lane < counts_ref[p], types_ref[p : p + 1, :], -1)
        gathered[me_t, p : p + 1, 0:atoms] = off[0:1, :] * (cells_x - 1)
        gathered[me_t, p : p + 1, atoms : 2 * atoms] = by + off[1:2, :] * SPAN
        gathered[me_t, p : p + 1, 2 * atoms : 3 * atoms] = bz + off[2:3, :] * SPAN
        gathered[me_t, p : p + 1, 3 * atoms : 4 * atoms] = kind.astype(jnp.float32)

    pl.semaphore_wait(barrier, tiles - 1 + slabs - 1)

    def tile_copy(i, block):
        return pltpu.make_async_remote_copy(
            src_ref=gathered.at[block],
            dst_ref=gathered.at[block],
            send_sem=tile_send.at[i],
            recv_sem=tile_recv.at[i],
            device_id=(me_s, lax.rem(me_t + i, tiles)),
            device_id_type=MESH,
        )

    for i in range(1, tiles):
        tile_copy(i, me_t).start()

    col = route_ref[...]
    row = to_row(col, group)
    before = (iota((group, group), 0) < iota((group, group), 1)) & (col == row)
    rank = jnp.sum(before.astype(jnp.int32), axis=0, keepdims=True)
    hits = iota((slots, group), 0) == row * cap + rank
    pick = hits.astype(jnp.float32).astype(jnp.bfloat16)
    empty = 1.0 - jnp.sum(hits.astype(jnp.float32), axis=1, keepdims=True)

    for i in range(1, tiles):
        tile_copy(i, lax.rem(me_t - i + tiles, tiles)).wait_recv()

    data = gathered[...].reshape(group, ROWS * atoms)
    high = data.astype(jnp.bfloat16)
    rest = data - high.astype(jnp.float32)
    mid = rest.astype(jnp.bfloat16)
    low = (rest - mid.astype(jnp.float32)).astype(jnp.bfloat16)
    dot = functools.partial(jnp.dot, preferred_element_type=jnp.float32)
    routed = (dot(pick, high) + dot(pick, mid)) + dot(pick, low)
    shift = jnp.where(iota((1, ROWS * atoms), 1) // atoms == 1, FAR, 0.0)
    routed = routed + empty * shift
    for s in range(slabs):
        outgoing[s] = routed[s * cap : (s + 1) * cap, :]

    def slab_copy(i, src, dst):
        return pltpu.make_async_remote_copy(
            src_ref=outgoing.at[src],
            dst_ref=incoming_ref.at[dst],
            send_sem=slab_send.at[i],
            recv_sem=slab_recv.at[i],
            device_id=(lax.rem(me_s + i, slabs), me_t),
            device_id_type=MESH,
        )

    @pl.loop(1, slabs)
    def _(i):
        slab_copy(i, lax.rem(me_s + i, slabs), me_s).start()

    incoming_ref[me_s] = outgoing[me_s]
    for i in range(1, tiles):
        tile_copy(i, me_t).wait_send()

    @pl.loop(1, slabs)
    def _(i):
        slab_copy(i, lax.rem(me_s + i, slabs), lax.rem(me_s - i + slabs, slabs)).wait()


def score_kernel(
    cells_x, cells_y, cells_z, chans,
    incoming_ref, gt_ref, table_ref, part_ref,
    lines_of, weights, coefs, sums, plan_v, plan_s, plan_sem,
):
    me_t = lax.axis_index("tile")
    slabs, cap, wide = incoming_ref.shape
    atoms = wide // ROWS
    slots = slabs * cap
    kinds = table_ref.shape[1]
    window = SPAN + 2
    first_row = me_t * cells_y
    first_f = first_row.astype(jnp.float32)

    for r in range(ROWS):
        lines_of[r] = incoming_ref[:, :, r * atoms : (r + 1) * atoms].reshape(slots, atoms)
    ys = lines_of[1]
    zs = lines_of[2]
    y_min = jnp.min(ys, axis=1, keepdims=True)
    y_max = jnp.max(ys, axis=1, keepdims=True)
    z_min = jnp.min(zs, axis=1, keepdims=True)
    start = jnp.minimum((z_min * 0.5).astype(jnp.int32) * 2, cells_z - window)
    near = ((y_max > first_f - 1.0) & (y_min < first_f + cells_y)).astype(jnp.int32)
    near_row = to_row(near, slots)
    up = iota((slots, slots), 0)
    across = iota((slots, slots), 1)
    rank = jnp.sum(jnp.where(across < up, near_row, 0), axis=1, keepdims=True)
    chosen = (rank == across) & (near > 0)
    plan_v[0:1, :] = jnp.sum(jnp.where(chosen, up, 0), axis=0, keepdims=True)
    plan_v[1:2, :] = jnp.sum(jnp.where(chosen, start, 0), axis=0, keepdims=True)
    total = jnp.sum(jnp.broadcast_to(near, (slots, slots)), axis=0, keepdims=True)
    plan_v[2:3, :] = total
    copy = pltpu.make_async_copy(plan_v, plan_s, plan_sem)
    copy.start()
    for t in range(kinds):
        coefs[t] = jnp.broadcast_to(table_ref[:, t : t + 1], (chans, atoms))
    sums[...] = jnp.zeros_like(sums)
    rows_f = (iota((cells_y, atoms), 0) + first_row).astype(jnp.float32)
    cells_f = iota((window, chans, atoms), 0)
    copy.wait()

    @pl.loop(0, plan_s[2, 0])
    def _(i):
        slot = plan_s[0, i]
        z_first = plan_s[1, i]
        x, y, z, kind = (lines_of[r, pl.ds(slot, 1), :] for r in range(ROWS))
        wy = jnp.maximum(1.0 - jnp.abs(y - rows_f), 0.0)
        for cx in range(cells_x):
            wx = jnp.maximum(1.0 - jnp.abs(x - cx), 0.0)
            w = wx * wy
            high = w.astype(jnp.bfloat16)
            low = (w - high.astype(jnp.float32)).astype(jnp.bfloat16)
            weights[cx * cells_y : (cx + 1) * cells_y, 0:atoms] = high
            weights[cx * cells_y : (cx + 1) * cells_y, atoms : 2 * atoms] = low
        lines = pl.ds(pl.multiple_of(z_first * chans, 2 * chans), window * chans)
        mixed = jnp.dot(gt_ref[lines, :], weights[...], preferred_element_type=jnp.float32)
        mixed = (mixed[:, 0:atoms] + mixed[:, atoms:]).reshape(window, chans, atoms)
        wz = jnp.maximum(1.0 - jnp.abs(z[None] - (cells_f + z_first).astype(jnp.float32)), 0.0)
        value = jnp.sum(wz * mixed, axis=0)
        coef = jnp.zeros((chans, atoms), jnp.float32)
        for t in range(kinds):
            coef = jnp.where(kind == t, coefs[t], coef)
        sums[pl.ds(slot, 1), :] = jnp.sum(value * coef, axis=0, keepdims=True)

    part_ref[...] = to_row(jnp.sum(sums[...], axis=1, keepdims=True), slots)


def return_kernel(slabs, tiles, cap, part_ref, route_ref, out_ref, landed, ranks, send, recv):
    me_s = lax.axis_index("slab")
    me_t = lax.axis_index("tile")
    group = route_ref.shape[0]
    poses = group // tiles
    slots = slabs * cap
    devices = slabs * tiles
    me = me_s * tiles + me_t

    barrier = pltpu.get_barrier_semaphore()

    @pl.loop(1, devices)
    def _(i):
        other = lax.rem(me + i, devices)
        pl.semaphore_signal(
            barrier, inc=1, device_id=(other // tiles, lax.rem(other, tiles)), device_id_type=MESH
        )

    col = route_ref[...]
    row = to_row(col, group)
    before = (iota((group, group), 1) < iota((group, group), 0)) & (col == row)
    ranks[...] = jnp.sum(before.astype(jnp.int32), axis=1, keepdims=True)
    pl.semaphore_wait(barrier, devices - 1)

    def copy(i, block):
        other = lax.rem(me + i, devices)
        return pltpu.make_async_remote_copy(
            src_ref=part_ref,
            dst_ref=landed.at[block],
            send_sem=send.at[i],
            recv_sem=recv.at[i],
            device_id=(other // tiles, lax.rem(other, tiles)),
            device_id_type=MESH,
        )

    @pl.loop(1, devices)
    def _(i):
        copy(i, me).start()

    landed[me] = part_ref[...]

    @pl.loop(1, devices)
    def _(i):
        copy(i, lax.rem(me - i + devices, devices)).wait()

    mine = pl.ds(pl.multiple_of(me_t * poses, poses), poses)
    target = route_ref[mine, :]
    rank = ranks[mine, :]
    found = jnp.zeros((poses, slots), jnp.float32)
    for s in range(slabs):
        line = landed[s * tiles]
        for t in range(1, tiles):
            line = line + landed[s * tiles + t]
        found = jnp.where(target == s, line, found)
    found = jnp.where(iota((poses, slots), 1) == me_s * cap + rank, found, 0.0)
    out_ref[...] = jnp.sum(found, axis=1, keepdims=True)


def vmem():
    return pl.BlockSpec(memory_space=pltpu.VMEM)


def smem():
    return pl.BlockSpec(memory_space=pltpu.SMEM)


def body(grid, type_table, counts, types, offsets, route, base_y, base_z):
    slabs = lax.axis_size("slab")
    tiles = lax.axis_size("tile")
    poses, atoms = types.shape
    kinds, chans = type_table.shape
    cells_x, cells_y, wide_z = grid.shape
    cells_z = wide_z // chans
    cap = max(2, 8 * poses // slabs)
    slots = slabs * cap
    devices = slabs * tiles
    dma = pltpu.SemaphoreType.DMA
    incoming = pl.pallas_call(
        functools.partial(exchange_kernel, slabs, tiles, cap, cells_x),
        out_shape=jax.ShapeDtypeStruct((slabs, cap, ROWS * atoms), jnp.float32),
        in_specs=[smem(), smem(), smem(), vmem(), vmem(), vmem()],
        out_specs=vmem(),
        scratch_shapes=[
            pltpu.VMEM((tiles, poses, ROWS * atoms), jnp.float32),
            pltpu.VMEM((slabs, cap, ROWS * atoms), jnp.float32),
            dma((tiles,)), dma((tiles,)), dma((slabs,)), dma((slabs,)),
        ],
        compiler_params=pltpu.CompilerParams(collective_id=0, has_side_effects=True),
        name="exchange",
    )(counts, base_y, base_z, route, types, offsets)
    gt = grid.reshape(cells_x * cells_y, wide_z).T
    part = pl.pallas_call(
        functools.partial(score_kernel, cells_x, cells_y, cells_z, chans),
        out_shape=jax.ShapeDtypeStruct((1, slots), jnp.float32),
        in_specs=[vmem(), vmem(), vmem()],
        out_specs=vmem(),
        scratch_shapes=[
            pltpu.VMEM((ROWS, slots, atoms), jnp.float32),
            pltpu.VMEM((cells_x * cells_y, 2 * atoms), jnp.bfloat16),
            pltpu.VMEM((kinds, chans, atoms), jnp.float32),
            pltpu.VMEM((slots, atoms), jnp.float32),
            pltpu.VMEM((8, slots), jnp.int32),
            pltpu.SMEM((8, slots), jnp.int32),
            dma,
        ],
        name="score",
    )(incoming, gt, type_table.T)
    out = pl.pallas_call(
        functools.partial(return_kernel, slabs, tiles, cap),
        out_shape=jax.ShapeDtypeStruct((poses, 1), jnp.float32),
        in_specs=[vmem(), vmem()],
        out_specs=vmem(),
        scratch_shapes=[
            pltpu.VMEM((devices, 1, slots), jnp.float32),
            pltpu.VMEM((tiles * poses, 1), jnp.int32),
            dma((devices,)), dma((devices,)),
        ],
        compiler_params=pltpu.CompilerParams(collective_id=1, has_side_effects=True),
        name="giveback",
    )(part, route)
    return out[:, 0] / counts.astype(jnp.float32)


def solution(mesh):
    in_specs = (
        P("slab", "tile", None),
        P(),
        P(("slab", "tile")),
        P(("slab", "tile"), None),
        P(("slab", "tile"), None, None),
        P("slab", None),
        P(("slab", "tile")),
        P(("slab", "tile")),
    )
    out_specs = P(("slab", "tile"))
    return jax.shard_map(body, mesh=mesh, in_specs=in_specs, out_specs=out_specs, check_vma=False)
```

```python
import functools

import jax
import jax.numpy as jnp
from jax import lax
from jax.experimental import pallas as pl
from jax.experimental.pallas import tpu as pltpu
from jax.sharding import PartitionSpec as P

SPAN = 32
ROWS = 4
FAR = -1.0e6
MESH = pl.DeviceIdType.MESH


def iota(shape, dim):
    return lax.broadcasted_iota(jnp.int32, shape, dim)


def to_row(col, count):
    eye = iota((count, count), 0) == iota((count, count), 1)
    return jnp.sum(jnp.where(eye, col, 0), axis=0, keepdims=True)


def to_col(row, count):
    eye = iota((count, count), 0) == iota((count, count), 1)
    return jnp.sum(jnp.where(eye, row, 0), axis=1, keepdims=True)


def hat(distance):
    return jnp.maximum(1.0 - jnp.abs(distance), 0.0)


def greet(barrier, slabs, tiles):
    me_s = lax.axis_index("slab")
    me_t = lax.axis_index("tile")

    @pl.loop(1, slabs)
    def _(i):
        pl.semaphore_signal(
            barrier, inc=1, device_id=(lax.rem(me_s + i, slabs), me_t), device_id_type=MESH
        )

    for i in range(1, tiles):
        pl.semaphore_signal(
            barrier, inc=1, device_id=(me_s, lax.rem(me_t + i, tiles)), device_id_type=MESH
        )


def exchange_kernel(
    slabs, tiles, cap, cells_x,
    counts_ref, base_y_ref, base_z_ref, route_ref, types_ref, offsets_ref, grid_ref,
    incoming_ref, gt_ref,
    gathered, outgoing, grid_v, gt_v, tile_send, tile_recv, slab_send, slab_recv, grid_sem, gt_sem,
):
    me_s = lax.axis_index("slab")
    me_t = lax.axis_index("tile")
    poses, atoms = types_ref.shape
    group = tiles * poses
    slots = slabs * cap

    barrier = pltpu.get_barrier_semaphore()
    greet(barrier, slabs, tiles)
    grid_in = pltpu.make_async_copy(grid_ref, grid_v, grid_sem)
    grid_in.start()

    lane = iota((1, atoms), 1)
    for p in range(poses):
        by = jnp.full((1, atoms), base_y_ref[p], jnp.int32).astype(jnp.float32)
        bz = jnp.full((1, atoms), base_z_ref[p], jnp.int32).astype(jnp.float32)
        kind = jnp.where(lane < counts_ref[p], types_ref[p : p + 1, :], -1)
        gathered[me_t, p : p + 1, 0:atoms] = offsets_ref[0, p : p + 1, :] * (cells_x - 1)
        gathered[me_t, p : p + 1, atoms : 2 * atoms] = by + offsets_ref[1, p : p + 1, :] * SPAN
        gathered[me_t, p : p + 1, 2 * atoms : 3 * atoms] = bz + offsets_ref[2, p : p + 1, :] * SPAN
        gathered[me_t, p : p + 1, 3 * atoms : 4 * atoms] = kind.astype(jnp.float32)

    pl.semaphore_wait(barrier, tiles - 1 + slabs - 1)

    def tile_copy(i, block):
        return pltpu.make_async_remote_copy(
            src_ref=gathered.at[block],
            dst_ref=gathered.at[block],
            send_sem=tile_send.at[i],
            recv_sem=tile_recv.at[i],
            device_id=(me_s, lax.rem(me_t + i, tiles)),
            device_id_type=MESH,
        )

    for i in range(1, tiles):
        tile_copy(i, me_t).start()

    row = route_ref[...]
    col = to_col(row, group)
    before = (iota((group, group), 0) < iota((group, group), 1)) & (col == row)
    rank = jnp.sum(before.astype(jnp.int32), axis=0, keepdims=True)
    hits = iota((slots, group), 0) == row * cap + rank
    pick = hits.astype(jnp.float32).astype(jnp.bfloat16)
    empty = 1.0 - jnp.sum(hits.astype(jnp.float32), axis=1, keepdims=True)

    for i in range(1, tiles):
        tile_copy(i, lax.rem(me_t - i + tiles, tiles)).wait_recv()

    data = gathered[...].reshape(group, ROWS * atoms)
    high = data.astype(jnp.bfloat16)
    rest = data - high.astype(jnp.float32)
    mid = rest.astype(jnp.bfloat16)
    low = (rest - mid.astype(jnp.float32)).astype(jnp.bfloat16)
    dot = functools.partial(jnp.dot, preferred_element_type=jnp.float32)
    routed = (dot(pick, high) + dot(pick, mid)) + dot(pick, low)
    shift = jnp.where(iota((1, ROWS * atoms), 1) // atoms == 1, FAR, 0.0)
    routed = routed + empty * shift
    for s in range(slabs):
        outgoing[s] = routed[s * cap : (s + 1) * cap, :]

    def slab_copy(i, src, dst):
        return pltpu.make_async_remote_copy(
            src_ref=outgoing.at[src],
            dst_ref=incoming_ref.at[dst],
            send_sem=slab_send.at[i],
            recv_sem=slab_recv.at[i],
            device_id=(lax.rem(me_s + i, slabs), me_t),
            device_id_type=MESH,
        )

    @pl.loop(1, slabs)
    def _(i):
        slab_copy(i, lax.rem(me_s + i, slabs), me_s).start()

    incoming_ref[me_s] = outgoing[me_s]
    for i in range(1, tiles):
        tile_copy(i, me_t).wait_send()

    grid_in.wait()
    lanes = grid_v.shape[1]
    for c in range(0, lanes, 128):
        gt_v[c : c + 128, :] = grid_v[:, c : c + 128].T
    gt_out = pltpu.make_async_copy(gt_v, gt_ref, gt_sem)
    gt_out.start()

    @pl.loop(1, slabs)
    def _(i):
        slab_copy(i, lax.rem(me_s + i, slabs), lax.rem(me_s - i + slabs, slabs)).wait()

    gt_out.wait()


def score_kernel(
    cells_x, cells_y, cells_z, chans,
    incoming_ref, gt_ref, table_ref, part_ref,
    lines_of, weights, hats_z, hats_x, coefs, sums, gt_v, plan_v, plan_s, plan_sem, gt_sem,
):
    me_t = lax.axis_index("tile")
    slabs, cap, wide = incoming_ref.shape
    atoms = wide // ROWS
    slots = slabs * cap
    kinds = table_ref.shape[1]
    window = SPAN + 2
    first_row = me_t * cells_y
    first_f = first_row.astype(jnp.float32)

    gt_in = pltpu.make_async_copy(gt_ref, gt_v, gt_sem)
    gt_in.start()
    for r in range(ROWS):
        lines_of[r] = incoming_ref[:, :, r * atoms : (r + 1) * atoms].reshape(slots, atoms)
    ys = lines_of[1]
    zs = lines_of[2]
    y_min = jnp.min(ys, axis=1, keepdims=True)
    y_max = jnp.max(ys, axis=1, keepdims=True)
    z_min = jnp.min(zs, axis=1, keepdims=True)
    start = jnp.minimum((z_min * 0.5).astype(jnp.int32) * 2, cells_z - window)
    near = ((y_max > first_f - 1.0) & (y_min < first_f + cells_y)).astype(jnp.int32)
    near_row = to_row(near, slots)
    up = iota((slots, slots), 0)
    across = iota((slots, slots), 1)
    rank = jnp.sum(jnp.where(across < up, near_row, 0), axis=1, keepdims=True)
    chosen = (rank == across) & (near > 0)
    plan_v[0:1, :] = jnp.sum(jnp.where(chosen, up, 0), axis=0, keepdims=True)
    plan_v[1:2, :] = jnp.sum(jnp.where(chosen, start, 0), axis=0, keepdims=True)
    total = jnp.sum(jnp.broadcast_to(near, (slots, slots)), axis=0, keepdims=True)
    plan_v[2:3, :] = total
    copy = pltpu.make_async_copy(plan_v, plan_s, plan_sem)
    copy.start()
    for t in range(kinds):
        coefs[t] = jnp.broadcast_to(table_ref[:, t : t + 1], (chans, atoms))
    sums[...] = jnp.zeros_like(sums)
    rows_f = (iota((cells_y, atoms), 0) + first_row).astype(jnp.float32)
    deep = hats_z.shape[1]
    copy.wait()
    count = plan_s[2, 0]

    def build(i, b):
        slot = plan_s[0, i]
        x = lines_of[0, pl.ds(slot, 1), :]
        y = lines_of[1, pl.ds(slot, 1), :]
        hats_x[b] = hat(x - iota((cells_x, atoms), 0).astype(jnp.float32))
        wy = hat(y - rows_f)
        for cx in range(cells_x):
            w = hats_x[b, cx : cx + 1, :] * wy
            high = w.astype(jnp.bfloat16)
            low = (w - high.astype(jnp.float32)).astype(jnp.bfloat16)
            weights[b, cx * cells_y : (cx + 1) * cells_y, 0:atoms] = high
            weights[b, cx * cells_y : (cx + 1) * cells_y, atoms : 2 * atoms] = low

    def finish(i, b):
        slot = plan_s[0, i]
        z_first = plan_s[1, i]
        z = lines_of[2, pl.ds(slot, 1), :]
        kind = lines_of[3, pl.ds(slot, 1), :]
        hats_z[b] = hat(z - (iota((deep, atoms), 0) + z_first).astype(jnp.float32))
        lines = pl.ds(pl.multiple_of(z_first * chans, 2 * chans), window * chans)
        mixed = jnp.dot(gt_v[lines, :], weights[b], preferred_element_type=jnp.float32)
        value = jnp.zeros((chans, atoms), jnp.float32)
        for j in range(window):
            part = slice(j * chans, (j + 1) * chans)
            both = mixed[part, 0:atoms] + mixed[part, atoms:]
            value = value + hats_z[b, j : j + 1, :] * both
        coef = jnp.zeros((chans, atoms), jnp.float32)
        for t in range(kinds):
            coef = jnp.where(kind == t, coefs[t], coef)
        sums[pl.ds(slot, 1), :] = jnp.sum(value * coef, axis=0, keepdims=True)

    build(0, 0)
    gt_in.wait()

    @pl.loop(0, (count + 1) // 2)
    def _(pair):
        first = 2 * pair
        second = jnp.minimum(first + 1, count - 1)
        third = jnp.minimum(first + 2, count - 1)
        build(second, 1)
        finish(first, 0)
        build(third, 0)
        finish(second, 1)

    part_ref[...] = to_row(jnp.sum(sums[...], axis=1, keepdims=True), slots)


def return_kernel(
    slabs, tiles, cap,
    part_ref, route_ref, counts_ref, out_ref,
    near, landed, line, ranks, tile_send, tile_recv, slab_send, slab_recv,
):
    me_s = lax.axis_index("slab")
    me_t = lax.axis_index("tile")
    group = route_ref.shape[1]
    poses = group // tiles
    slots = slabs * cap

    barrier = pltpu.get_barrier_semaphore()
    greet(barrier, slabs, tiles)
    row = route_ref[...]
    col = to_col(row, group)
    before = (iota((group, group), 1) < iota((group, group), 0)) & (col == row)
    ranks[0] = jnp.sum(before.astype(jnp.int32), axis=1, keepdims=True)
    ranks[1] = col
    pl.semaphore_wait(barrier, tiles - 1 + slabs - 1)

    def tile_copy(i, block):
        return pltpu.make_async_remote_copy(
            src_ref=part_ref,
            dst_ref=near.at[block],
            send_sem=tile_send.at[i],
            recv_sem=tile_recv.at[i],
            device_id=(me_s, lax.rem(me_t + i, tiles)),
            device_id_type=MESH,
        )

    for i in range(1, tiles):
        tile_copy(i, me_t).start()
    near[me_t] = part_ref[...]
    mine = pl.ds(pl.multiple_of(me_t * poses, poses), poses)
    rank = ranks[0, mine, :]
    target = ranks[1, mine, :]
    for i in range(1, tiles):
        tile_copy(i, lax.rem(me_t - i + tiles, tiles)).wait()
    total = near[0]
    for t in range(1, tiles):
        total = total + near[t]
    line[...] = total

    def slab_copy(i, block):
        return pltpu.make_async_remote_copy(
            src_ref=line,
            dst_ref=landed.at[block],
            send_sem=slab_send.at[i],
            recv_sem=slab_recv.at[i],
            device_id=(lax.rem(me_s + i, slabs), me_t),
            device_id_type=MESH,
        )

    @pl.loop(1, slabs)
    def _(i):
        slab_copy(i, me_s).start()

    landed[me_s] = total

    @pl.loop(1, slabs)
    def _(i):
        slab_copy(i, lax.rem(me_s - i + slabs, slabs)).wait()

    found = jnp.zeros((poses, slots), jnp.float32)
    for s in range(slabs):
        found = jnp.where(target == s, landed[s], found)
    found = jnp.where(iota((poses, slots), 1) == me_s * cap + rank, found, 0.0)
    energy = to_row(jnp.sum(found, axis=1, keepdims=True), poses)
    out_ref[...] = energy / counts_ref[...].astype(jnp.float32)


def vmem():
    return pl.BlockSpec(memory_space=pltpu.VMEM)


def smem():
    return pl.BlockSpec(memory_space=pltpu.SMEM)


def body(grid, type_table, counts, types, offsets, route, base_y, base_z):
    slabs = lax.axis_size("slab")
    tiles = lax.axis_size("tile")
    poses, atoms = types.shape
    kinds, chans = type_table.shape
    cells_x, cells_y, wide_z = grid.shape
    cells_z = wide_z // chans
    cap = max(2, 8 * poses // slabs)
    slots = slabs * cap
    devices = slabs * tiles
    dma = pltpu.SemaphoreType.DMA
    flat = grid.reshape(cells_x * cells_y, wide_z)
    route_row = route.reshape(1, tiles * poses)
    anywhere = pl.BlockSpec(memory_space=pl.ANY)
    incoming, gt = pl.pallas_call(
        functools.partial(exchange_kernel, slabs, tiles, cap, cells_x),
        out_shape=(
            jax.ShapeDtypeStruct((slabs, cap, ROWS * atoms), jnp.float32),
            jax.ShapeDtypeStruct((wide_z, cells_x * cells_y), grid.dtype),
        ),
        in_specs=[smem(), smem(), smem(), vmem(), vmem(), vmem(), anywhere],
        out_specs=(vmem(), anywhere),
        scratch_shapes=[
            pltpu.VMEM((tiles, poses, ROWS * atoms), jnp.float32),
            pltpu.VMEM((slabs, cap, ROWS * atoms), jnp.float32),
            pltpu.VMEM((cells_x * cells_y, wide_z), grid.dtype),
            pltpu.VMEM((wide_z, cells_x * cells_y), grid.dtype),
            dma((tiles,)), dma((tiles,)), dma((slabs,)), dma((slabs,)), dma, dma,
        ],
        compiler_params=pltpu.CompilerParams(collective_id=0, has_side_effects=True),
        name="exchange",
    )(counts, base_y, base_z, route_row, types, jnp.swapaxes(offsets, 0, 1), flat)
    part = pl.pallas_call(
        functools.partial(score_kernel, cells_x, cells_y, cells_z, chans),
        out_shape=jax.ShapeDtypeStruct((1, slots), jnp.float32),
        in_specs=[vmem(), anywhere, vmem()],
        out_specs=vmem(),
        scratch_shapes=[
            pltpu.VMEM((ROWS, slots, atoms), jnp.float32),
            pltpu.VMEM((2, cells_x * cells_y, 2 * atoms), jnp.bfloat16),
            pltpu.VMEM((2, -(-(SPAN + 2) // 8) * 8, atoms), jnp.float32),
            pltpu.VMEM((2, cells_x, atoms), jnp.float32),
            pltpu.VMEM((kinds, chans, atoms), jnp.float32),
            pltpu.VMEM((slots, atoms), jnp.float32),
            pltpu.VMEM((wide_z, cells_x * cells_y), grid.dtype),
            pltpu.VMEM((8, slots), jnp.int32),
            pltpu.SMEM((8, slots), jnp.int32),
            dma, dma,
        ],
        name="score",
    )(incoming, gt, type_table.T)
    out = pl.pallas_call(
        functools.partial(return_kernel, slabs, tiles, cap),
        out_shape=jax.ShapeDtypeStruct((1, poses), jnp.float32),
        in_specs=[vmem(), vmem(), vmem()],
        out_specs=vmem(),
        scratch_shapes=[
            pltpu.VMEM((tiles, 1, slots), jnp.float32),
            pltpu.VMEM((slabs, 1, slots), jnp.float32),
            pltpu.VMEM((1, slots), jnp.float32),
            pltpu.VMEM((2, tiles * poses, 1), jnp.int32),
            dma((tiles,)), dma((tiles,)), dma((slabs,)), dma((slabs,)),
        ],
        compiler_params=pltpu.CompilerParams(collective_id=1, has_side_effects=True),
        name="giveback",
    )(part, route_row, counts.reshape(1, poses))
    return out.reshape(poses)


def solution(mesh):
    in_specs = (
        P("slab", "tile", None),
        P(),
        P(("slab", "tile")),
        P(("slab", "tile"), None),
        P(("slab", "tile"), None, None),
        P("slab", None),
        P(("slab", "tile")),
        P(("slab", "tile")),
    )
    out_specs = P(("slab", "tile"))
    return jax.shard_map(body, mesh=mesh, in_specs=in_specs, out_specs=out_specs, check_vma=False)
```

```python
import functools

import jax
import jax.numpy as jnp
from jax import lax
from jax.experimental import pallas as pl
from jax.experimental.pallas import tpu as pltpu
from jax.sharding import PartitionSpec as P

SPAN = 32
ROWS = 4
FAR = -1.0e6
MESH = pl.DeviceIdType.MESH


def iota(shape, dim):
    return lax.broadcasted_iota(jnp.int32, shape, dim)


def to_row(col, count):
    eye = iota((count, count), 0) == iota((count, count), 1)
    return jnp.sum(jnp.where(eye, col, 0), axis=0, keepdims=True)


def to_col(row, count):
    eye = iota((count, count), 0) == iota((count, count), 1)
    return jnp.sum(jnp.where(eye, row, 0), axis=1, keepdims=True)


def hat(distance):
    return jnp.maximum(1.0 - jnp.abs(distance), 0.0)


def greet(barrier, slabs, tiles):
    me_s = lax.axis_index("slab")
    me_t = lax.axis_index("tile")

    @pl.loop(1, slabs)
    def _(i):
        pl.semaphore_signal(
            barrier, inc=1, device_id=(lax.rem(me_s + i, slabs), me_t), device_id_type=MESH
        )

    for i in range(1, tiles):
        pl.semaphore_signal(
            barrier, inc=1, device_id=(me_s, lax.rem(me_t + i, tiles)), device_id_type=MESH
        )


def exchange_kernel(
    slabs, tiles, cap, cells_x,
    counts_any, base_y_any, base_z_any, route_any, types_any, offsets_any, grid_ref,
    incoming_ref, gt_ref,
    counts_ref, base_y_ref, base_z_ref, route_ref, types_ref, offsets_ref,
    gathered, outgoing, grid_v, gt_v,
    tile_send, tile_recv, slab_send, slab_recv, grid_sem, gt_sem, load_sem,
):
    me_s = lax.axis_index("slab")
    me_t = lax.axis_index("tile")
    poses, atoms = types_any.shape
    group = tiles * poses
    slots = slabs * cap

    barrier = pltpu.get_barrier_semaphore()
    greet(barrier, slabs, tiles)
    grid_in = pltpu.make_async_copy(grid_ref, grid_v, grid_sem)
    loads = [
        pltpu.make_async_copy(src, dst, load_sem.at[i])
        for i, (src, dst) in enumerate(
            (
                (counts_any, counts_ref),
                (base_y_any, base_y_ref),
                (base_z_any, base_z_ref),
                (types_any, types_ref),
                (offsets_any, offsets_ref),
                (route_any, route_ref),
            )
        )
    ]
    for load in loads:
        load.start()
    grid_in.start()
    for load in loads:
        load.wait()

    lane = iota((1, atoms), 1)
    for p in range(poses):
        by = jnp.full((1, atoms), base_y_ref[p], jnp.int32).astype(jnp.float32)
        bz = jnp.full((1, atoms), base_z_ref[p], jnp.int32).astype(jnp.float32)
        kind = jnp.where(lane < counts_ref[p], types_ref[p : p + 1, :], -1)
        gathered[me_t, p : p + 1, 0:atoms] = offsets_ref[0, p : p + 1, :] * (cells_x - 1)
        gathered[me_t, p : p + 1, atoms : 2 * atoms] = by + offsets_ref[1, p : p + 1, :] * SPAN
        gathered[me_t, p : p + 1, 2 * atoms : 3 * atoms] = bz + offsets_ref[2, p : p + 1, :] * SPAN
        gathered[me_t, p : p + 1, 3 * atoms : 4 * atoms] = kind.astype(jnp.float32)

    pl.semaphore_wait(barrier, tiles - 1 + slabs - 1)

    def tile_copy(i, block):
        return pltpu.make_async_remote_copy(
            src_ref=gathered.at[block],
            dst_ref=gathered.at[block],
            send_sem=tile_send.at[i],
            recv_sem=tile_recv.at[i],
            device_id=(me_s, lax.rem(me_t + i, tiles)),
            device_id_type=MESH,
        )

    for i in range(1, tiles):
        tile_copy(i, me_t).start()

    row = route_ref[...]
    col = to_col(row, group)
    before = (iota((group, group), 0) < iota((group, group), 1)) & (col == row)
    rank = jnp.sum(before.astype(jnp.int32), axis=0, keepdims=True)
    hits = iota((slots, group), 0) == row * cap + rank
    pick = hits.astype(jnp.float32).astype(jnp.bfloat16)
    empty = 1.0 - jnp.sum(hits.astype(jnp.float32), axis=1, keepdims=True)

    for i in range(1, tiles):
        tile_copy(i, lax.rem(me_t - i + tiles, tiles)).wait_recv()

    data = gathered[...].reshape(group, ROWS * atoms)
    high = data.astype(jnp.bfloat16)
    rest = data - high.astype(jnp.float32)
    mid = rest.astype(jnp.bfloat16)
    low = (rest - mid.astype(jnp.float32)).astype(jnp.bfloat16)
    dot = functools.partial(jnp.dot, preferred_element_type=jnp.float32)
    routed = (dot(pick, high) + dot(pick, mid)) + dot(pick, low)
    shift = jnp.where(iota((1, ROWS * atoms), 1) // atoms == 1, FAR, 0.0)
    routed = routed + empty * shift
    for s in range(slabs):
        outgoing[s] = routed[s * cap : (s + 1) * cap, :]

    def slab_copy(i, src, dst):
        return pltpu.make_async_remote_copy(
            src_ref=outgoing.at[src],
            dst_ref=incoming_ref.at[dst],
            send_sem=slab_send.at[i],
            recv_sem=slab_recv.at[i],
            device_id=(lax.rem(me_s + i, slabs), me_t),
            device_id_type=MESH,
        )

    @pl.loop(1, slabs)
    def _(i):
        slab_copy(i, lax.rem(me_s + i, slabs), me_s).start()

    incoming_ref[me_s] = outgoing[me_s]
    for i in range(1, tiles):
        tile_copy(i, me_t).wait_send()

    grid_in.wait()
    parts, lanes, deep = gt_v.shape
    step = deep // cells_x
    for h in range(parts):
        for c in range(0, lanes, 128):
            block = grid_v[:, h * step : (h + 1) * step, c : c + 128]
            gt_v[h, c : c + 128, :] = block.reshape(deep, 128).T
    gt_out = pltpu.make_async_copy(gt_v, gt_ref, gt_sem)
    gt_out.start()

    @pl.loop(1, slabs)
    def _(i):
        slab_copy(i, lax.rem(me_s + i, slabs), lax.rem(me_s - i + slabs, slabs)).wait()

    gt_out.wait()


def score_kernel(
    cells_x, cells_y, cells_z, chans,
    incoming_ref, gt_ref, table_ref, part_ref,
    lines_of, weights, hats_z, hats_x, coefs, sums, gt_v, plan_v, plan_s, plan_sem, gt_sem,
):
    me_t = lax.axis_index("tile")
    slabs, cap, wide = incoming_ref.shape
    atoms = wide // ROWS
    slots = slabs * cap
    kinds = table_ref.shape[1]
    window = SPAN + 2
    parts, _, depth = gt_ref.shape
    step = cells_y // parts
    first_row = me_t * cells_y

    gt_in = pltpu.make_async_copy(gt_ref, gt_v, gt_sem)
    gt_in.start()
    for r in range(ROWS):
        lines_of[r] = incoming_ref[:, :, r * atoms : (r + 1) * atoms].reshape(slots, atoms)
    ys = lines_of[1]
    zs = lines_of[2]
    y_min = jnp.min(ys, axis=1, keepdims=True)
    y_max = jnp.max(ys, axis=1, keepdims=True)
    z_min = jnp.min(zs, axis=1, keepdims=True)
    start = jnp.minimum((z_min * 0.5).astype(jnp.int32) * 2, cells_z - window)
    up = iota((slots, slots), 0)
    across = iota((slots, slots), 1)
    wide_up = iota((slots, parts * slots), 0)
    wide_across = iota((slots, parts * slots), 1)
    used = jnp.zeros((1, 1), jnp.int32)
    rows = [jnp.zeros((1, parts * slots), jnp.int32) for _ in range(3)]
    for h in range(parts):
        low_f = (first_row + h * step).astype(jnp.float32)
        near = ((y_max > low_f - 1.0) & (y_min < low_f + step)).astype(jnp.int32)
        near_row = to_row(near, slots)
        rank = jnp.sum(jnp.where(across < up, near_row, 0), axis=1, keepdims=True)
        chosen = (rank + used == wide_across) & (near > 0)
        for n, item in enumerate((wide_up, start, h)):
            rows[n] = rows[n] + jnp.sum(jnp.where(chosen, item, 0), axis=0, keepdims=True)
        used = used + jnp.sum(near, axis=0, keepdims=True)
    for n in range(3):
        plan_v[n : n + 1, :] = rows[n]
    plan_v[3:4, :] = jnp.broadcast_to(used, (1, parts * slots))
    copy = pltpu.make_async_copy(plan_v, plan_s, plan_sem)
    copy.start()
    for t in range(kinds):
        coefs[t] = jnp.broadcast_to(table_ref[:, t : t + 1], (chans, atoms))
    sums[...] = jnp.zeros_like(sums)
    rows_i = iota((step, atoms), 0) + first_row
    deep = hats_z.shape[1]
    copy.wait()
    count = plan_s[3, 0]

    def build(i, b):
        slot = plan_s[0, i]
        x = lines_of[0, pl.ds(slot, 1), :]
        y = lines_of[1, pl.ds(slot, 1), :]
        hats_x[b] = hat(x - iota((cells_x, atoms), 0).astype(jnp.float32))
        wy = hat(y - (rows_i + plan_s[2, i] * step).astype(jnp.float32))
        for cx in range(cells_x):
            w = hats_x[b, cx : cx + 1, :] * wy
            high = w.astype(jnp.bfloat16)
            low = (w - high.astype(jnp.float32)).astype(jnp.bfloat16)
            weights[b, cx * step : (cx + 1) * step, 0:atoms] = high
            weights[b, cx * step : (cx + 1) * step, atoms : 2 * atoms] = low

    def finish(i, b):
        slot = plan_s[0, i]
        z_first = plan_s[1, i]
        h = plan_s[2, i]
        z = lines_of[2, pl.ds(slot, 1), :]
        kind = lines_of[3, pl.ds(slot, 1), :]
        hats_z[b] = hat(z - (iota((deep, atoms), 0) + z_first).astype(jnp.float32))
        lines = pl.ds(pl.multiple_of(z_first * chans, 2 * chans), window * chans)
        mixed = jnp.dot(gt_v[h, lines, :], weights[b], preferred_element_type=jnp.float32)
        value = jnp.zeros((chans, atoms), jnp.float32)
        for j in range(window):
            part = slice(j * chans, (j + 1) * chans)
            both = mixed[part, 0:atoms] + mixed[part, atoms:]
            value = value + hats_z[b, j : j + 1, :] * both
        coef = jnp.zeros((chans, atoms), jnp.float32)
        for t in range(kinds):
            coef = jnp.where(kind == t, coefs[t], coef)
        sums[h, pl.ds(slot, 1), :] = jnp.sum(value * coef, axis=0, keepdims=True)

    build(0, 0)
    gt_in.wait()

    @pl.loop(0, (count + 1) // 2)
    def _(pair):
        first = 2 * pair
        second = jnp.minimum(first + 1, count - 1)
        third = jnp.minimum(first + 2, count - 1)
        build(second, 1)
        finish(first, 0)
        build(third, 0)
        finish(second, 1)

    part_ref[...] = to_row(jnp.sum(jnp.sum(sums[...], axis=0), axis=1, keepdims=True), slots)


def return_kernel(
    slabs, tiles, cap,
    part_any, route_any, out_ref,
    part_ref, route_ref, near, landed, line, ranks,
    tile_send, tile_recv, slab_send, slab_recv, load_sem,
):
    me_s = lax.axis_index("slab")
    me_t = lax.axis_index("tile")
    group = route_any.shape[1]
    poses = group // tiles
    slots = slabs * cap

    barrier = pltpu.get_barrier_semaphore()
    greet(barrier, slabs, tiles)
    part_in = pltpu.make_async_copy(part_any, part_ref, load_sem.at[0])
    part_in.start()
    route_in = pltpu.make_async_copy(route_any, route_ref, load_sem.at[1])
    route_in.start()
    route_in.wait()
    row = route_ref[...]
    col = to_col(row, group)
    before = (iota((group, group), 1) < iota((group, group), 0)) & (col == row)
    ranks[0] = jnp.sum(before.astype(jnp.int32), axis=1, keepdims=True)
    ranks[1] = col
    part_in.wait()
    pl.semaphore_wait(barrier, tiles - 1 + slabs - 1)

    def tile_copy(i, block):
        return pltpu.make_async_remote_copy(
            src_ref=part_ref,
            dst_ref=near.at[block],
            send_sem=tile_send.at[i],
            recv_sem=tile_recv.at[i],
            device_id=(me_s, lax.rem(me_t + i, tiles)),
            device_id_type=MESH,
        )

    for i in range(1, tiles):
        tile_copy(i, me_t).start()
    near[me_t] = part_ref[...]
    mine = pl.ds(pl.multiple_of(me_t * poses, poses), poses)
    rank = ranks[0, mine, :]
    target = ranks[1, mine, :]
    for i in range(1, tiles):
        tile_copy(i, lax.rem(me_t - i + tiles, tiles)).wait()
    total = near[0]
    for t in range(1, tiles):
        total = total + near[t]
    line[...] = total

    def slab_copy(i, block):
        return pltpu.make_async_remote_copy(
            src_ref=line,
            dst_ref=landed.at[block],
            send_sem=slab_send.at[i],
            recv_sem=slab_recv.at[i],
            device_id=(lax.rem(me_s + i, slabs), me_t),
            device_id_type=MESH,
        )

    @pl.loop(1, slabs)
    def _(i):
        slab_copy(i, me_s).start()

    landed[me_s] = total

    @pl.loop(1, slabs)
    def _(i):
        slab_copy(i, lax.rem(me_s - i + slabs, slabs)).wait()

    found = jnp.zeros((poses, slots), jnp.float32)
    for s in range(slabs):
        found = jnp.where(target == s, landed[s], found)
    found = jnp.where(iota((poses, slots), 1) == me_s * cap + rank, found, 0.0)
    out_ref[...] = to_row(jnp.sum(found, axis=1, keepdims=True), poses)


def vmem():
    return pl.BlockSpec(memory_space=pltpu.VMEM)


def body(grid, type_table, counts, types, offsets, route, base_y, base_z):
    slabs = lax.axis_size("slab")
    tiles = lax.axis_size("tile")
    poses, atoms = types.shape
    kinds, chans = type_table.shape
    cells_x, cells_y, wide_z = grid.shape
    cells_z = wide_z // chans
    cap = max(2, 8 * poses // slabs)
    slots = slabs * cap
    devices = slabs * tiles
    dma = pltpu.SemaphoreType.DMA
    step = min(cells_y, SPAN)
    parts = cells_y // step
    depth = cells_x * step
    route_row = route.reshape(1, tiles * poses)
    anywhere = pl.BlockSpec(memory_space=pl.ANY)
    incoming, gt = pl.pallas_call(
        functools.partial(exchange_kernel, slabs, tiles, cap, cells_x),
        out_shape=(
            jax.ShapeDtypeStruct((slabs, cap, ROWS * atoms), jnp.float32),
            jax.ShapeDtypeStruct((parts, wide_z, depth), grid.dtype),
        ),
        in_specs=[anywhere] * 7,
        out_specs=(vmem(), anywhere),
        scratch_shapes=[
            pltpu.SMEM((poses,), jnp.int32),
            pltpu.SMEM((poses,), jnp.int32),
            pltpu.SMEM((poses,), jnp.int32),
            pltpu.VMEM((1, tiles * poses), jnp.int32),
            pltpu.VMEM((poses, atoms), jnp.int32),
            pltpu.VMEM((3, poses, atoms), jnp.float32),
            pltpu.VMEM((tiles, poses, ROWS * atoms), jnp.float32),
            pltpu.VMEM((slabs, cap, ROWS * atoms), jnp.float32),
            pltpu.VMEM(grid.shape, grid.dtype),
            pltpu.VMEM((parts, wide_z, depth), grid.dtype),
            dma((tiles,)), dma((tiles,)), dma((slabs,)), dma((slabs,)), dma, dma, dma((6,)),
        ],
        compiler_params=pltpu.CompilerParams(collective_id=0, has_side_effects=True),
        name="exchange",
    )(counts, base_y, base_z, route_row, types, jnp.swapaxes(offsets, 0, 1), grid)
    part = pl.pallas_call(
        functools.partial(score_kernel, cells_x, cells_y, cells_z, chans),
        out_shape=jax.ShapeDtypeStruct((1, slots), jnp.float32),
        in_specs=[vmem(), anywhere, vmem()],
        out_specs=vmem(),
        scratch_shapes=[
            pltpu.VMEM((ROWS, slots, atoms), jnp.float32),
            pltpu.VMEM((2, depth, 2 * atoms), jnp.bfloat16),
            pltpu.VMEM((2, -(-(SPAN + 2) // 8) * 8, atoms), jnp.float32),
            pltpu.VMEM((2, cells_x, atoms), jnp.float32),
            pltpu.VMEM((kinds, chans, atoms), jnp.float32),
            pltpu.VMEM((parts, slots, atoms), jnp.float32),
            pltpu.VMEM((parts, wide_z, depth), grid.dtype),
            pltpu.VMEM((8, parts * slots), jnp.int32),
            pltpu.SMEM((8, parts * slots), jnp.int32),
            dma, dma,
        ],
        name="score",
    )(incoming, gt, type_table.T)
    out = pl.pallas_call(
        functools.partial(return_kernel, slabs, tiles, cap),
        out_shape=jax.ShapeDtypeStruct((1, poses), jnp.float32),
        in_specs=[anywhere, anywhere],
        out_specs=vmem(),
        scratch_shapes=[
            pltpu.VMEM((1, slots), jnp.float32),
            pltpu.VMEM((1, tiles * poses), jnp.int32),
            pltpu.VMEM((tiles, 1, slots), jnp.float32),
            pltpu.VMEM((slabs, 1, slots), jnp.float32),
            pltpu.VMEM((1, slots), jnp.float32),
            pltpu.VMEM((2, tiles * poses, 1), jnp.int32),
            dma((tiles,)), dma((tiles,)), dma((slabs,)), dma((slabs,)), dma((2,)),
        ],
        compiler_params=pltpu.CompilerParams(collective_id=1, has_side_effects=True),
        name="giveback",
    )(part, route_row)
    return out.reshape(poses) / counts.astype(jnp.float32)


def solution(mesh):
    in_specs = (
        P("slab", "tile", None),
        P(),
        P(("slab", "tile")),
        P(("slab", "tile"), None),
        P(("slab", "tile"), None, None),
        P("slab", None),
        P(("slab", "tile")),
        P(("slab", "tile")),
    )
    out_specs = P(("slab", "tile"))
    return jax.shard_map(body, mesh=mesh, in_specs=in_specs, out_specs=out_specs, check_vma=False)
```

```python
import functools

import jax
import jax.numpy as jnp
from jax import lax
from jax.experimental import pallas as pl
from jax.experimental.pallas import tpu as pltpu
from jax.sharding import PartitionSpec as P

SPAN = 32
ROWS = 4
DEEP = 4
FAR = -1.0e6
MESH = pl.DeviceIdType.MESH


def iota(shape, dim):
    return lax.broadcasted_iota(jnp.int32, shape, dim)


def to_row(col, count):
    eye = iota((count, count), 0) == iota((count, count), 1)
    return jnp.sum(jnp.where(eye, col, 0), axis=0, keepdims=True)


def to_col(row, count):
    eye = iota((count, count), 0) == iota((count, count), 1)
    return jnp.sum(jnp.where(eye, row, 0), axis=1, keepdims=True)


def hat(distance):
    return jnp.maximum(1.0 - jnp.abs(distance), 0.0)


def greet(barrier, slabs, tiles):
    me_s = lax.axis_index("slab")
    me_t = lax.axis_index("tile")

    @pl.loop(1, slabs)
    def _(i):
        pl.semaphore_signal(
            barrier, inc=1, device_id=(lax.rem(me_s + i, slabs), me_t), device_id_type=MESH
        )

    for i in range(1, tiles):
        pl.semaphore_signal(
            barrier, inc=1, device_id=(me_s, lax.rem(me_t + i, tiles)), device_id_type=MESH
        )


def exchange_kernel(
    slabs, tiles, cap, cells_x,
    counts_any, base_y_any, base_z_any, route_any, types_any, offsets_any, grid_ref,
    incoming_ref, gt_ref,
    counts_ref, base_y_ref, base_z_ref, route_ref, types_ref, offsets_ref,
    gathered, outgoing, grid_v, gt_v,
    tile_send, tile_recv, slab_send, slab_recv, grid_sem, gt_sem, load_sem,
):
    me_s = lax.axis_index("slab")
    me_t = lax.axis_index("tile")
    poses, atoms = types_any.shape
    group = tiles * poses
    slots = slabs * cap

    barrier = pltpu.get_barrier_semaphore()
    greet(barrier, slabs, tiles)
    grid_in = pltpu.make_async_copy(grid_ref, grid_v, grid_sem)
    loads = [
        pltpu.make_async_copy(src, dst, load_sem.at[i])
        for i, (src, dst) in enumerate(
            (
                (counts_any, counts_ref),
                (base_y_any, base_y_ref),
                (base_z_any, base_z_ref),
                (types_any, types_ref),
                (offsets_any, offsets_ref),
                (route_any, route_ref),
            )
        )
    ]
    for load in loads:
        load.start()
    grid_in.start()
    for load in loads:
        load.wait()

    lane = iota((1, atoms), 1)
    for p in range(poses):
        by = jnp.full((1, atoms), base_y_ref[p], jnp.int32).astype(jnp.float32)
        bz = jnp.full((1, atoms), base_z_ref[p], jnp.int32).astype(jnp.float32)
        kind = jnp.where(lane < counts_ref[p], types_ref[p : p + 1, :], -1)
        gathered[me_t, p : p + 1, 0:atoms] = offsets_ref[0, p : p + 1, :] * (cells_x - 1)
        gathered[me_t, p : p + 1, atoms : 2 * atoms] = by + offsets_ref[1, p : p + 1, :] * SPAN
        gathered[me_t, p : p + 1, 2 * atoms : 3 * atoms] = bz + offsets_ref[2, p : p + 1, :] * SPAN
        gathered[me_t, p : p + 1, 3 * atoms : 4 * atoms] = kind.astype(jnp.float32)

    pl.semaphore_wait(barrier, tiles - 1 + slabs - 1)

    def tile_copy(i, block):
        return pltpu.make_async_remote_copy(
            src_ref=gathered.at[block],
            dst_ref=gathered.at[block],
            send_sem=tile_send.at[i],
            recv_sem=tile_recv.at[i],
            device_id=(me_s, lax.rem(me_t + i, tiles)),
            device_id_type=MESH,
        )

    for i in range(1, tiles):
        tile_copy(i, me_t).start()

    row = route_ref[...]
    col = to_col(row, group)
    before = (iota((group, group), 0) < iota((group, group), 1)) & (col == row)
    rank = jnp.sum(before.astype(jnp.int32), axis=0, keepdims=True)
    hits = iota((slots, group), 0) == row * cap + rank
    pick = hits.astype(jnp.float32).astype(jnp.bfloat16)
    empty = 1.0 - jnp.sum(hits.astype(jnp.float32), axis=1, keepdims=True)

    for i in range(1, tiles):
        tile_copy(i, lax.rem(me_t - i + tiles, tiles)).wait_recv()

    data = gathered[...].reshape(group, ROWS * atoms)
    high = data.astype(jnp.bfloat16)
    rest = data - high.astype(jnp.float32)
    mid = rest.astype(jnp.bfloat16)
    low = (rest - mid.astype(jnp.float32)).astype(jnp.bfloat16)
    dot = functools.partial(jnp.dot, preferred_element_type=jnp.float32)
    routed = (dot(pick, high) + dot(pick, mid)) + dot(pick, low)
    shift = jnp.where(iota((1, ROWS * atoms), 1) // atoms == 1, FAR, 0.0)
    routed = routed + empty * shift
    for s in range(slabs):
        outgoing[s] = routed[s * cap : (s + 1) * cap, :]

    def slab_copy(i, src, dst):
        return pltpu.make_async_remote_copy(
            src_ref=outgoing.at[src],
            dst_ref=incoming_ref.at[dst],
            send_sem=slab_send.at[i],
            recv_sem=slab_recv.at[i],
            device_id=(lax.rem(me_s + i, slabs), me_t),
            device_id_type=MESH,
        )

    @pl.loop(1, slabs)
    def _(i):
        slab_copy(i, lax.rem(me_s + i, slabs), me_s).start()

    incoming_ref[me_s] = outgoing[me_s]
    for i in range(1, tiles):
        tile_copy(i, me_t).wait_send()

    grid_in.wait()
    parts, lanes, deep = gt_v.shape
    step = deep // cells_x
    for h in range(parts):
        for c in range(0, lanes, 128):
            block = grid_v[:, h * step : (h + 1) * step, c : c + 128]
            gt_v[h, c : c + 128, :] = block.reshape(deep, 128).T
    gt_out = pltpu.make_async_copy(gt_v, gt_ref, gt_sem)
    gt_out.start()

    @pl.loop(1, slabs)
    def _(i):
        slab_copy(i, lax.rem(me_s + i, slabs), lax.rem(me_s - i + slabs, slabs)).wait()

    gt_out.wait()


def score_kernel(
    cells_x, cells_y, cells_z, chans,
    incoming_ref, gt_ref, table_ref, part_ref,
    lines_of, weights, hats_z, hats_x, coefs, sums, gt_v, plan_v, plan_s, plan_sem, gt_sem,
):
    me_t = lax.axis_index("tile")
    slabs, cap, wide = incoming_ref.shape
    atoms = wide // ROWS
    slots = slabs * cap
    kinds = table_ref.shape[1]
    window = SPAN + 2
    parts, _, depth = gt_ref.shape
    step = cells_y // parts
    first_row = me_t * cells_y

    gt_in = pltpu.make_async_copy(gt_ref, gt_v, gt_sem)
    gt_in.start()
    for r in range(ROWS):
        lines_of[r] = incoming_ref[:, :, r * atoms : (r + 1) * atoms].reshape(slots, atoms)
    ys = lines_of[1]
    zs = lines_of[2]
    y_min = jnp.min(ys, axis=1, keepdims=True)
    y_max = jnp.max(ys, axis=1, keepdims=True)
    z_min = jnp.min(zs, axis=1, keepdims=True)
    start = jnp.minimum((z_min * 0.5).astype(jnp.int32) * 2, cells_z - window)
    up = iota((slots, slots), 0)
    across = iota((slots, slots), 1)
    wide_up = iota((slots, parts * slots), 0)
    wide_across = iota((slots, parts * slots), 1)
    used = jnp.zeros((1, 1), jnp.int32)
    rows = [jnp.zeros((1, parts * slots), jnp.int32) for _ in range(3)]
    for h in range(parts):
        low_f = (first_row + h * step).astype(jnp.float32)
        near = ((y_max > low_f - 1.0) & (y_min < low_f + step)).astype(jnp.int32)
        near_row = to_row(near, slots)
        rank = jnp.sum(jnp.where(across < up, near_row, 0), axis=1, keepdims=True)
        chosen = (rank + used == wide_across) & (near > 0)
        for n, item in enumerate((wide_up, start, h)):
            rows[n] = rows[n] + jnp.sum(jnp.where(chosen, item, 0), axis=0, keepdims=True)
        used = used + jnp.sum(near, axis=0, keepdims=True)
    for n in range(3):
        plan_v[n : n + 1, :] = rows[n]
    plan_v[3:4, :] = jnp.broadcast_to(used, (1, parts * slots))
    copy = pltpu.make_async_copy(plan_v, plan_s, plan_sem)
    copy.start()
    for t in range(kinds):
        coefs[t] = jnp.broadcast_to(table_ref[:, t : t + 1], (chans, atoms))
    sums[...] = jnp.zeros_like(sums)
    rows_i = iota((step, atoms), 0) + first_row
    deep = hats_z.shape[1]
    copy.wait()
    count = plan_s[3, 0]

    def build(i, b):
        slot = plan_s[0, i]
        x = lines_of[0, pl.ds(slot, 1), :]
        y = lines_of[1, pl.ds(slot, 1), :]
        hats_x[b] = hat(x - iota((cells_x, atoms), 0).astype(jnp.float32))
        wy = hat(y - (rows_i + plan_s[2, i] * step).astype(jnp.float32))
        for cx in range(cells_x):
            w = hats_x[b, cx : cx + 1, :] * wy
            high = w.astype(jnp.bfloat16)
            low = (w - high.astype(jnp.float32)).astype(jnp.bfloat16)
            weights[b, cx * step : (cx + 1) * step, 0:atoms] = high
            weights[b, cx * step : (cx + 1) * step, atoms : 2 * atoms] = low

    def finish(i, b):
        slot = plan_s[0, i]
        z_first = plan_s[1, i]
        h = plan_s[2, i]
        z = lines_of[2, pl.ds(slot, 1), :]
        kind = lines_of[3, pl.ds(slot, 1), :]
        hats_z[b] = hat(z - (iota((deep, atoms), 0) + z_first).astype(jnp.float32))
        lines = pl.ds(pl.multiple_of(z_first * chans, 2 * chans), window * chans)
        mixed = jnp.dot(gt_v[h, lines, :], weights[b], preferred_element_type=jnp.float32)
        value = jnp.zeros((chans, atoms), jnp.float32)
        for j in range(window):
            part = slice(j * chans, (j + 1) * chans)
            both = mixed[part, 0:atoms] + mixed[part, atoms:]
            value = value + hats_z[b, j : j + 1, :] * both
        coef = jnp.zeros((chans, atoms), jnp.float32)
        for t in range(kinds):
            coef = jnp.where(kind == t, coefs[t], coef)
        sums[h, pl.ds(slot, 1), :] = jnp.sum(value * coef, axis=0, keepdims=True)

    build(0, 0)
    gt_in.wait()

    @pl.loop(0, (count + DEEP - 1) // DEEP)
    def _(turn):
        units = [jnp.minimum(DEEP * turn + n, count - 1) for n in range(DEEP + 1)]
        for n in range(DEEP):
            build(units[n + 1], (n + 1) % DEEP)
            finish(units[n], n)

    part_ref[...] = to_row(jnp.sum(jnp.sum(sums[...], axis=0), axis=1, keepdims=True), slots)


def return_kernel(
    slabs, tiles, cap,
    part_any, route_any, out_ref,
    part_ref, route_ref, near, landed, line, ranks,
    tile_send, tile_recv, slab_send, slab_recv, load_sem,
):
    me_s = lax.axis_index("slab")
    me_t = lax.axis_index("tile")
    group = route_any.shape[1]
    poses = group // tiles
    slots = slabs * cap

    barrier = pltpu.get_barrier_semaphore()
    greet(barrier, slabs, tiles)
    part_in = pltpu.make_async_copy(part_any, part_ref, load_sem.at[0])
    part_in.start()
    route_in = pltpu.make_async_copy(route_any, route_ref, load_sem.at[1])
    route_in.start()
    route_in.wait()
    row = route_ref[...]
    col = to_col(row, group)
    before = (iota((group, group), 1) < iota((group, group), 0)) & (col == row)
    ranks[0] = jnp.sum(before.astype(jnp.int32), axis=1, keepdims=True)
    ranks[1] = col
    part_in.wait()
    pl.semaphore_wait(barrier, tiles - 1 + slabs - 1)

    def tile_copy(i, block):
        return pltpu.make_async_remote_copy(
            src_ref=part_ref,
            dst_ref=near.at[block],
            send_sem=tile_send.at[i],
            recv_sem=tile_recv.at[i],
            device_id=(me_s, lax.rem(me_t + i, tiles)),
            device_id_type=MESH,
        )

    for i in range(1, tiles):
        tile_copy(i, me_t).start()
    near[me_t] = part_ref[...]
    mine = pl.ds(pl.multiple_of(me_t * poses, poses), poses)
    rank = ranks[0, mine, :]
    target = ranks[1, mine, :]
    for i in range(1, tiles):
        tile_copy(i, lax.rem(me_t - i + tiles, tiles)).wait()
    total = near[0]
    for t in range(1, tiles):
        total = total + near[t]
    line[...] = total

    def slab_copy(i, block):
        return pltpu.make_async_remote_copy(
            src_ref=line,
            dst_ref=landed.at[block],
            send_sem=slab_send.at[i],
            recv_sem=slab_recv.at[i],
            device_id=(lax.rem(me_s + i, slabs), me_t),
            device_id_type=MESH,
        )

    @pl.loop(1, slabs)
    def _(i):
        slab_copy(i, me_s).start()

    landed[me_s] = total

    @pl.loop(1, slabs)
    def _(i):
        slab_copy(i, lax.rem(me_s - i + slabs, slabs)).wait()

    found = jnp.zeros((poses, slots), jnp.float32)
    for s in range(slabs):
        found = jnp.where(target == s, landed[s], found)
    found = jnp.where(iota((poses, slots), 1) == me_s * cap + rank, found, 0.0)
    out_ref[...] = to_row(jnp.sum(found, axis=1, keepdims=True), poses)


def vmem():
    return pl.BlockSpec(memory_space=pltpu.VMEM)


def body(grid, type_table, counts, types, offsets, route, base_y, base_z):
    slabs = lax.axis_size("slab")
    tiles = lax.axis_size("tile")
    poses, atoms = types.shape
    kinds, chans = type_table.shape
    cells_x, cells_y, wide_z = grid.shape
    cells_z = wide_z // chans
    cap = max(2, 8 * poses // slabs)
    slots = slabs * cap
    devices = slabs * tiles
    dma = pltpu.SemaphoreType.DMA
    step = min(cells_y, SPAN)
    parts = cells_y // step
    depth = cells_x * step
    route_row = route.reshape(1, tiles * poses)
    anywhere = pl.BlockSpec(memory_space=pl.ANY)
    incoming, gt = pl.pallas_call(
        functools.partial(exchange_kernel, slabs, tiles, cap, cells_x),
        out_shape=(
            jax.ShapeDtypeStruct((slabs, cap, ROWS * atoms), jnp.float32),
            jax.ShapeDtypeStruct((parts, wide_z, depth), grid.dtype),
        ),
        in_specs=[anywhere] * 7,
        out_specs=(vmem(), anywhere),
        scratch_shapes=[
            pltpu.SMEM((poses,), jnp.int32),
            pltpu.SMEM((poses,), jnp.int32),
            pltpu.SMEM((poses,), jnp.int32),
            pltpu.VMEM((1, tiles * poses), jnp.int32),
            pltpu.VMEM((poses, atoms), jnp.int32),
            pltpu.VMEM((3, poses, atoms), jnp.float32),
            pltpu.VMEM((tiles, poses, ROWS * atoms), jnp.float32),
            pltpu.VMEM((slabs, cap, ROWS * atoms), jnp.float32),
            pltpu.VMEM(grid.shape, grid.dtype),
            pltpu.VMEM((parts, wide_z, depth), grid.dtype),
            dma((tiles,)), dma((tiles,)), dma((slabs,)), dma((slabs,)), dma, dma, dma((6,)),
        ],
        compiler_params=pltpu.CompilerParams(collective_id=0, has_side_effects=True),
        name="exchange",
    )(counts, base_y, base_z, route_row, types, jnp.swapaxes(offsets, 0, 1), grid)
    part = pl.pallas_call(
        functools.partial(score_kernel, cells_x, cells_y, cells_z, chans),
        out_shape=jax.ShapeDtypeStruct((1, slots), jnp.float32),
        in_specs=[vmem(), anywhere, vmem()],
        out_specs=vmem(),
        scratch_shapes=[
            pltpu.VMEM((ROWS, slots, atoms), jnp.float32),
            pltpu.VMEM((DEEP, depth, 2 * atoms), jnp.bfloat16),
            pltpu.VMEM((DEEP, -(-(SPAN + 2) // 8) * 8, atoms), jnp.float32),
            pltpu.VMEM((DEEP, cells_x, atoms), jnp.float32),
            pltpu.VMEM((kinds, chans, atoms), jnp.float32),
            pltpu.VMEM((parts, slots, atoms), jnp.float32),
            pltpu.VMEM((parts, wide_z, depth), grid.dtype),
            pltpu.VMEM((8, parts * slots), jnp.int32),
            pltpu.SMEM((8, parts * slots), jnp.int32),
            dma, dma,
        ],
        name="score",
    )(incoming, gt, type_table.T)
    out = pl.pallas_call(
        functools.partial(return_kernel, slabs, tiles, cap),
        out_shape=jax.ShapeDtypeStruct((1, poses), jnp.float32),
        in_specs=[anywhere, anywhere],
        out_specs=vmem(),
        scratch_shapes=[
            pltpu.VMEM((1, slots), jnp.float32),
            pltpu.VMEM((1, tiles * poses), jnp.int32),
            pltpu.VMEM((tiles, 1, slots), jnp.float32),
            pltpu.VMEM((slabs, 1, slots), jnp.float32),
            pltpu.VMEM((1, slots), jnp.float32),
            pltpu.VMEM((2, tiles * poses, 1), jnp.int32),
            dma((tiles,)), dma((tiles,)), dma((slabs,)), dma((slabs,)), dma((2,)),
        ],
        compiler_params=pltpu.CompilerParams(collective_id=1, has_side_effects=True),
        name="giveback",
    )(part, route_row)
    return out.reshape(poses) / counts.astype(jnp.float32)


def solution(mesh):
    in_specs = (
        P("slab", "tile", None),
        P(),
        P(("slab", "tile")),
        P(("slab", "tile"), None),
        P(("slab", "tile"), None, None),
        P("slab", None),
        P(("slab", "tile")),
        P(("slab", "tile")),
    )
    out_specs = P(("slab", "tile"))
    return jax.shard_map(body, mesh=mesh, in_specs=in_specs, out_specs=out_specs, check_vma=False)
```

```python
import functools

import jax
import jax.numpy as jnp
from jax import lax
from jax.experimental import pallas as pl
from jax.experimental.pallas import tpu as pltpu
from jax.sharding import PartitionSpec as P

SPAN = 32
ROWS = 4
DEEP = 8
FAR = -1.0e6
MESH = pl.DeviceIdType.MESH


def iota(shape, dim):
    return lax.broadcasted_iota(jnp.int32, shape, dim)


def to_row(col, count):
    eye = iota((count, count), 0) == iota((count, count), 1)
    return jnp.sum(jnp.where(eye, col, 0), axis=0, keepdims=True)


def to_col(row, count):
    eye = iota((count, count), 0) == iota((count, count), 1)
    return jnp.sum(jnp.where(eye, row, 0), axis=1, keepdims=True)


def hat(distance):
    return jnp.maximum(1.0 - jnp.abs(distance), 0.0)


def greet(barrier, slabs, tiles):
    me_s = lax.axis_index("slab")
    me_t = lax.axis_index("tile")

    @pl.loop(1, slabs)
    def _(i):
        pl.semaphore_signal(
            barrier, inc=1, device_id=(lax.rem(me_s + i, slabs), me_t), device_id_type=MESH
        )

    for i in range(1, tiles):
        pl.semaphore_signal(
            barrier, inc=1, device_id=(me_s, lax.rem(me_t + i, tiles)), device_id_type=MESH
        )


def exchange_kernel(
    slabs, tiles, cap, cells_x,
    counts_any, base_y_any, base_z_any, route_any, types_any, offsets_any, grid_ref,
    incoming_ref, gt_ref,
    counts_ref, base_y_ref, base_z_ref, route_ref, types_ref, offsets_ref,
    gathered, outgoing, grid_v, gt_v,
    tile_send, tile_recv, slab_send, slab_recv, grid_sem, gt_sem, load_sem,
):
    me_s = lax.axis_index("slab")
    me_t = lax.axis_index("tile")
    poses, atoms = types_any.shape
    group = tiles * poses
    slots = slabs * cap

    barrier = pltpu.get_barrier_semaphore()
    greet(barrier, slabs, tiles)
    grid_in = pltpu.make_async_copy(grid_ref, grid_v, grid_sem)
    loads = [
        pltpu.make_async_copy(src, dst, load_sem.at[i])
        for i, (src, dst) in enumerate(
            (
                (counts_any, counts_ref),
                (base_y_any, base_y_ref),
                (base_z_any, base_z_ref),
                (types_any, types_ref),
                (offsets_any, offsets_ref),
                (route_any, route_ref),
            )
        )
    ]
    for load in loads:
        load.start()
    grid_in.start()
    for load in loads:
        load.wait()

    lane = iota((1, atoms), 1)
    for p in range(poses):
        by = jnp.full((1, atoms), base_y_ref[p], jnp.int32).astype(jnp.float32)
        bz = jnp.full((1, atoms), base_z_ref[p], jnp.int32).astype(jnp.float32)
        kind = jnp.where(lane < counts_ref[p], types_ref[p : p + 1, :], -1)
        gathered[me_t, p : p + 1, 0:atoms] = offsets_ref[0, p : p + 1, :] * (cells_x - 1)
        gathered[me_t, p : p + 1, atoms : 2 * atoms] = by + offsets_ref[1, p : p + 1, :] * SPAN
        gathered[me_t, p : p + 1, 2 * atoms : 3 * atoms] = bz + offsets_ref[2, p : p + 1, :] * SPAN
        gathered[me_t, p : p + 1, 3 * atoms : 4 * atoms] = kind.astype(jnp.float32)

    pl.semaphore_wait(barrier, tiles - 1 + slabs - 1)

    def tile_copy(i, block):
        return pltpu.make_async_remote_copy(
            src_ref=gathered.at[block],
            dst_ref=gathered.at[block],
            send_sem=tile_send.at[i],
            recv_sem=tile_recv.at[i],
            device_id=(me_s, lax.rem(me_t + i, tiles)),
            device_id_type=MESH,
        )

    for i in range(1, tiles):
        tile_copy(i, me_t).start()

    row = route_ref[...]
    col = to_col(row, group)
    before = (iota((group, group), 0) < iota((group, group), 1)) & (col == row)
    rank = jnp.sum(before.astype(jnp.int32), axis=0, keepdims=True)
    hits = iota((slots, group), 0) == row * cap + rank
    pick = hits.astype(jnp.float32).astype(jnp.bfloat16)
    empty = 1.0 - jnp.sum(hits.astype(jnp.float32), axis=1, keepdims=True)

    for i in range(1, tiles):
        tile_copy(i, lax.rem(me_t - i + tiles, tiles)).wait_recv()

    data = gathered[...].reshape(group, ROWS * atoms)
    high = data.astype(jnp.bfloat16)
    rest = data - high.astype(jnp.float32)
    mid = rest.astype(jnp.bfloat16)
    low = (rest - mid.astype(jnp.float32)).astype(jnp.bfloat16)
    dot = functools.partial(jnp.dot, preferred_element_type=jnp.float32)
    routed = (dot(pick, high) + dot(pick, mid)) + dot(pick, low)
    shift = jnp.where(iota((1, ROWS * atoms), 1) // atoms == 1, FAR, 0.0)
    routed = routed + empty * shift
    for s in range(slabs):
        outgoing[s] = routed[s * cap : (s + 1) * cap, :]

    def slab_copy(i, src, dst):
        return pltpu.make_async_remote_copy(
            src_ref=outgoing.at[src],
            dst_ref=incoming_ref.at[dst],
            send_sem=slab_send.at[i],
            recv_sem=slab_recv.at[i],
            device_id=(lax.rem(me_s + i, slabs), me_t),
            device_id_type=MESH,
        )

    @pl.loop(1, slabs)
    def _(i):
        slab_copy(i, lax.rem(me_s + i, slabs), me_s).start()

    incoming_ref[me_s] = outgoing[me_s]
    for i in range(1, tiles):
        tile_copy(i, me_t).wait_send()

    grid_in.wait()
    parts, lanes, deep = gt_v.shape
    step = deep // cells_x
    for h in range(parts):
        for c in range(0, lanes, 128):
            block = grid_v[:, h * step : (h + 1) * step, c : c + 128]
            gt_v[h, c : c + 128, :] = block.reshape(deep, 128).T
    gt_out = pltpu.make_async_copy(gt_v, gt_ref, gt_sem)
    gt_out.start()

    @pl.loop(1, slabs)
    def _(i):
        slab_copy(i, lax.rem(me_s + i, slabs), lax.rem(me_s - i + slabs, slabs)).wait()

    gt_out.wait()


def score_kernel(
    cells_x, cells_y, cells_z, chans,
    incoming_ref, gt_ref, table_ref, part_ref,
    lines_of, weights, hats_z, hats_x, coefs, sums, gt_v, plan_v, plan_s, plan_sem, gt_sem,
):
    me_t = lax.axis_index("tile")
    slabs, cap, wide = incoming_ref.shape
    atoms = wide // ROWS
    slots = slabs * cap
    kinds = table_ref.shape[1]
    window = SPAN + 2
    parts, _, depth = gt_ref.shape
    step = cells_y // parts
    first_row = me_t * cells_y

    gt_in = pltpu.make_async_copy(gt_ref, gt_v, gt_sem)
    gt_in.start()
    for r in range(ROWS):
        lines_of[r] = incoming_ref[:, :, r * atoms : (r + 1) * atoms].reshape(slots, atoms)
    ys = lines_of[1]
    zs = lines_of[2]
    y_min = jnp.min(ys, axis=1, keepdims=True)
    y_max = jnp.max(ys, axis=1, keepdims=True)
    z_min = jnp.min(zs, axis=1, keepdims=True)
    start = jnp.minimum((z_min * 0.5).astype(jnp.int32) * 2, cells_z - window)
    up = iota((slots, slots), 0)
    across = iota((slots, slots), 1)
    wide_up = iota((slots, parts * slots), 0)
    wide_across = iota((slots, parts * slots), 1)
    used = jnp.zeros((1, 1), jnp.int32)
    rows = [jnp.zeros((1, parts * slots), jnp.int32) for _ in range(3)]
    for h in range(parts):
        low_f = (first_row + h * step).astype(jnp.float32)
        near = ((y_max > low_f - 1.0) & (y_min < low_f + step)).astype(jnp.int32)
        near_row = to_row(near, slots)
        rank = jnp.sum(jnp.where(across < up, near_row, 0), axis=1, keepdims=True)
        chosen = (rank + used == wide_across) & (near > 0)
        for n, item in enumerate((wide_up, start, h)):
            rows[n] = rows[n] + jnp.sum(jnp.where(chosen, item, 0), axis=0, keepdims=True)
        used = used + jnp.sum(near, axis=0, keepdims=True)
    for n in range(3):
        plan_v[n : n + 1, :] = rows[n]
    plan_v[3:4, :] = jnp.broadcast_to(used, (1, parts * slots))
    copy = pltpu.make_async_copy(plan_v, plan_s, plan_sem)
    copy.start()
    for t in range(kinds):
        coefs[t] = jnp.broadcast_to(table_ref[:, t : t + 1], (chans, atoms))
    sums[...] = jnp.zeros_like(sums)
    rows_i = iota((step, atoms), 0) + first_row
    deep = hats_z.shape[1]
    copy.wait()
    count = plan_s[3, 0]

    def build(i, b):
        slot = plan_s[0, i]
        x = lines_of[0, pl.ds(slot, 1), :]
        y = lines_of[1, pl.ds(slot, 1), :]
        hats_x[b] = hat(x - iota((cells_x, atoms), 0).astype(jnp.float32))
        wy = hat(y - (rows_i + plan_s[2, i] * step).astype(jnp.float32))
        for cx in range(cells_x):
            w = hats_x[b, cx : cx + 1, :] * wy
            high = w.astype(jnp.bfloat16)
            low = (w - high.astype(jnp.float32)).astype(jnp.bfloat16)
            weights[b, cx * step : (cx + 1) * step, 0:atoms] = high
            weights[b, cx * step : (cx + 1) * step, atoms : 2 * atoms] = low

    def finish(i, b):
        slot = plan_s[0, i]
        z_first = plan_s[1, i]
        h = plan_s[2, i]
        z = lines_of[2, pl.ds(slot, 1), :]
        kind = lines_of[3, pl.ds(slot, 1), :]
        hats_z[b] = hat(z - (iota((deep, atoms), 0) + z_first).astype(jnp.float32))
        lines = pl.ds(pl.multiple_of(z_first * chans, 2 * chans), window * chans)
        mixed = jnp.dot(gt_v[h, lines, :], weights[b], preferred_element_type=jnp.float32)
        value = jnp.zeros((chans, atoms), jnp.float32)
        for j in range(window):
            part = slice(j * chans, (j + 1) * chans)
            both = mixed[part, 0:atoms] + mixed[part, atoms:]
            value = value + hats_z[b, j : j + 1, :] * both
        coef = jnp.zeros((chans, atoms), jnp.float32)
        for t in range(kinds):
            coef = jnp.where(kind == t, coefs[t], coef)
        sums[h, pl.ds(slot, 1), :] = jnp.sum(value * coef, axis=0, keepdims=True)

    build(0, 0)
    gt_in.wait()

    @pl.loop(0, (count + DEEP - 1) // DEEP)
    def _(turn):
        units = [jnp.minimum(DEEP * turn + n, count - 1) for n in range(DEEP + 1)]
        for n in range(DEEP):
            build(units[n + 1], (n + 1) % DEEP)
            finish(units[n], n)

    part_ref[...] = to_row(jnp.sum(jnp.sum(sums[...], axis=0), axis=1, keepdims=True), slots)


def return_kernel(
    slabs, tiles, cap,
    part_any, route_any, out_ref,
    part_ref, route_ref, near, landed, line, ranks,
    tile_send, tile_recv, slab_send, slab_recv, load_sem,
):
    me_s = lax.axis_index("slab")
    me_t = lax.axis_index("tile")
    group = route_any.shape[1]
    poses = group // tiles
    slots = slabs * cap

    barrier = pltpu.get_barrier_semaphore()
    greet(barrier, slabs, tiles)
    part_in = pltpu.make_async_copy(part_any, part_ref, load_sem.at[0])
    part_in.start()
    route_in = pltpu.make_async_copy(route_any, route_ref, load_sem.at[1])
    route_in.start()
    route_in.wait()
    row = route_ref[...]
    col = to_col(row, group)
    before = (iota((group, group), 1) < iota((group, group), 0)) & (col == row)
    ranks[0] = jnp.sum(before.astype(jnp.int32), axis=1, keepdims=True)
    ranks[1] = col
    part_in.wait()
    pl.semaphore_wait(barrier, tiles - 1 + slabs - 1)

    def tile_copy(i, block):
        return pltpu.make_async_remote_copy(
            src_ref=part_ref,
            dst_ref=near.at[block],
            send_sem=tile_send.at[i],
            recv_sem=tile_recv.at[i],
            device_id=(me_s, lax.rem(me_t + i, tiles)),
            device_id_type=MESH,
        )

    for i in range(1, tiles):
        tile_copy(i, me_t).start()
    near[me_t] = part_ref[...]
    mine = pl.ds(pl.multiple_of(me_t * poses, poses), poses)
    rank = ranks[0, mine, :]
    target = ranks[1, mine, :]
    for i in range(1, tiles):
        tile_copy(i, lax.rem(me_t - i + tiles, tiles)).wait()
    total = near[0]
    for t in range(1, tiles):
        total = total + near[t]
    line[...] = total

    def slab_copy(i, block):
        return pltpu.make_async_remote_copy(
            src_ref=line,
            dst_ref=landed.at[block],
            send_sem=slab_send.at[i],
            recv_sem=slab_recv.at[i],
            device_id=(lax.rem(me_s + i, slabs), me_t),
            device_id_type=MESH,
        )

    @pl.loop(1, slabs)
    def _(i):
        slab_copy(i, me_s).start()

    landed[me_s] = total

    @pl.loop(1, slabs)
    def _(i):
        slab_copy(i, lax.rem(me_s - i + slabs, slabs)).wait()

    found = jnp.zeros((poses, slots), jnp.float32)
    for s in range(slabs):
        found = jnp.where(target == s, landed[s], found)
    found = jnp.where(iota((poses, slots), 1) == me_s * cap + rank, found, 0.0)
    out_ref[...] = to_row(jnp.sum(found, axis=1, keepdims=True), poses)


def vmem():
    return pl.BlockSpec(memory_space=pltpu.VMEM)


def body(grid, type_table, counts, types, offsets, route, base_y, base_z):
    slabs = lax.axis_size("slab")
    tiles = lax.axis_size("tile")
    poses, atoms = types.shape
    kinds, chans = type_table.shape
    cells_x, cells_y, wide_z = grid.shape
    cells_z = wide_z // chans
    cap = max(2, 8 * poses // slabs)
    slots = slabs * cap
    devices = slabs * tiles
    dma = pltpu.SemaphoreType.DMA
    step = min(cells_y, SPAN)
    parts = cells_y // step
    depth = cells_x * step
    route_row = route.reshape(1, tiles * poses)
    anywhere = pl.BlockSpec(memory_space=pl.ANY)
    incoming, gt = pl.pallas_call(
        functools.partial(exchange_kernel, slabs, tiles, cap, cells_x),
        out_shape=(
            jax.ShapeDtypeStruct((slabs, cap, ROWS * atoms), jnp.float32),
            jax.ShapeDtypeStruct((parts, wide_z, depth), grid.dtype),
        ),
        in_specs=[anywhere] * 7,
        out_specs=(vmem(), anywhere),
        scratch_shapes=[
            pltpu.SMEM((poses,), jnp.int32),
            pltpu.SMEM((poses,), jnp.int32),
            pltpu.SMEM((poses,), jnp.int32),
            pltpu.VMEM((1, tiles * poses), jnp.int32),
            pltpu.VMEM((poses, atoms), jnp.int32),
            pltpu.VMEM((3, poses, atoms), jnp.float32),
            pltpu.VMEM((tiles, poses, ROWS * atoms), jnp.float32),
            pltpu.VMEM((slabs, cap, ROWS * atoms), jnp.float32),
            pltpu.VMEM(grid.shape, grid.dtype),
            pltpu.VMEM((parts, wide_z, depth), grid.dtype),
            dma((tiles,)), dma((tiles,)), dma((slabs,)), dma((slabs,)), dma, dma, dma((6,)),
        ],
        compiler_params=pltpu.CompilerParams(collective_id=0, has_side_effects=True),
        name="exchange",
    )(counts, base_y, base_z, route_row, types, jnp.swapaxes(offsets, 0, 1), grid)
    part = pl.pallas_call(
        functools.partial(score_kernel, cells_x, cells_y, cells_z, chans),
        out_shape=jax.ShapeDtypeStruct((1, slots), jnp.float32),
        in_specs=[vmem(), anywhere, vmem()],
        out_specs=vmem(),
        scratch_shapes=[
            pltpu.VMEM((ROWS, slots, atoms), jnp.float32),
            pltpu.VMEM((DEEP, depth, 2 * atoms), jnp.bfloat16),
            pltpu.VMEM((DEEP, -(-(SPAN + 2) // 8) * 8, atoms), jnp.float32),
            pltpu.VMEM((DEEP, cells_x, atoms), jnp.float32),
            pltpu.VMEM((kinds, chans, atoms), jnp.float32),
            pltpu.VMEM((parts, slots, atoms), jnp.float32),
            pltpu.VMEM((parts, wide_z, depth), grid.dtype),
            pltpu.VMEM((8, parts * slots), jnp.int32),
            pltpu.SMEM((8, parts * slots), jnp.int32),
            dma, dma,
        ],
        name="score",
    )(incoming, gt, type_table.T)
    out = pl.pallas_call(
        functools.partial(return_kernel, slabs, tiles, cap),
        out_shape=jax.ShapeDtypeStruct((1, poses), jnp.float32),
        in_specs=[anywhere, anywhere],
        out_specs=vmem(),
        scratch_shapes=[
            pltpu.VMEM((1, slots), jnp.float32),
            pltpu.VMEM((1, tiles * poses), jnp.int32),
            pltpu.VMEM((tiles, 1, slots), jnp.float32),
            pltpu.VMEM((slabs, 1, slots), jnp.float32),
            pltpu.VMEM((1, slots), jnp.float32),
            pltpu.VMEM((2, tiles * poses, 1), jnp.int32),
            dma((tiles,)), dma((tiles,)), dma((slabs,)), dma((slabs,)), dma((2,)),
        ],
        compiler_params=pltpu.CompilerParams(collective_id=1, has_side_effects=True),
        name="giveback",
    )(part, route_row)
    return out.reshape(poses) / counts.astype(jnp.float32)


def solution(mesh):
    in_specs = (
        P("slab", "tile", None),
        P(),
        P(("slab", "tile")),
        P(("slab", "tile"), None),
        P(("slab", "tile"), None, None),
        P("slab", None),
        P(("slab", "tile")),
        P(("slab", "tile")),
    )
    out_specs = P(("slab", "tile"))
    return jax.shard_map(body, mesh=mesh, in_specs=in_specs, out_specs=out_specs, check_vma=False)
```
